32 devices in a mesh: dp: 2 (over y), ctx: 4 (over z), fsdp: 4 (over x, core).
Axes of the slice: x: 2, y: 2, z: 4, core: 2. Of those that a mesh axis runs over, the one named last changes fastest.
Arguments:
- layer_input: bfloat16 [8, 2048, 768], P(('dp', 'fsdp'), 'ctx'), may hold values from -6 to 6
- first_values: bfloat16 [8, 2048, 384], P(('dp', 'fsdp'), 'ctx'), may hold values from -6 to 6
- segment_ids: int32 [8, 2048], P(('dp', 'fsdp')), may hold values from 0 to 7, never falling along the last dimension, each value on 1 to 1024 neighbouring positions
- pairing: int32 [8], replicated, may hold values from 0 to 7, as said below
- norm_gains: bfloat16 [2, 768], P(None, 'fsdp'), may hold values from 0.099609375 to 1.8984375
- norm_biases: bfloat16 [2, 768], P(None, 'fsdp'), may hold values from -2 to 2
- w_qkv: bfloat16 [768, 1920], P('fsdp'), may hold values from -0.21875 to 0.21875
- w_out: bfloat16 [768, 768], P('fsdp'), may hold values from -0.875 to 0.875
- w_up: bfloat16 [768, 3072], P(None, 'fsdp'), may hold values from -0.21875 to 0.21875
- w_down: bfloat16 [3072, 768], P('fsdp'), may hold values from -0.109375 to 0.109375
- cotangent: bfloat16 [8, 2048, 768], P(('dp', 'fsdp'), 'ctx'), may hold values from -6 to 6
Outputs:
- layer_out: bfloat16 [8, 2048, 768], P(('dp', 'fsdp'), 'ctx')
- input_grad: float32 [8, 2048, 768], P(('dp', 'fsdp'), 'ctx')
- first_values_grad: float32 [8, 2048, 384], P(('dp', 'fsdp'), 'ctx')
- gains_grad: float32 [2, 768], P(None, 'fsdp')
- biases_grad: float32 [2, 768], P(None, 'fsdp')
- qkv_grad: float32 [768, 1920], P('fsdp')
- out_grad: float32 [768, 768], P('fsdp')
- up_grad: float32 [768, 3072], P(None, 'fsdp')
- down_grad: float32 [3072, 768], P('fsdp')
The draws below stay inside these ranges and needn't reach their ends.
Inputs may be any that keep to these rules, and one draw needn't show every extreme that they name: `segment_ids`: along each sequence the ids never fall; each document holds 1 to 1024 positions, one exactly that many. `pairing`: every block is named once; entries 2c and 2c + 1 name blocks b and 7 - b for some b, in either order.
All inputs are finite; a program needn't handle non-finite values.
Results may differ from the reference program's by a relative error of at most 0.019.
Values may be sent and summed in bfloat16 or wider, within the bound.
No kernel may reach another device: no remote copies, remote signals or barrier semaphores. Data moves between devices by JAX's collectives and lax.ppermute only.
A program may use at most 192 MiB of HBM per device.

```python
import math
import jax
import jax.numpy as jnp
import numpy as np
from jax import lax

D = 768
HEADS = 12
HD = 64
VH = 6
FF = 3072
BLOCK = 256
SEQ_LEN = 2048
NSEQ = 8
DOCS = 8


def draw_pairing(key, part):
    pair_count = SEQ_LEN // (2 * BLOCK)
    order = jax.random.permutation(key, pair_count).astype(jnp.int32)
    flips = jax.random.randint(jax.random.fold_in(key, 11), (pair_count,), 0, 2).astype(jnp.int32)
    mirror = 2 * pair_count - 1 - order
    first = jnp.where(flips == 1, mirror, order)
    second = jnp.where(flips == 1, order, mirror)
    return jnp.stack([first, second], axis=1).reshape(2 * pair_count).astype(jnp.int32)


def block_levels(own_key, dims, pieces, least, high):
    factor_of = 1.0
    for axis_at, blocks in pieces:
        heights = jax.random.uniform(jax.random.fold_in(jax.random.fold_in(own_key, 6), axis_at), (blocks,), jnp.float32, least / len(pieces), high / len(pieces))
        factor_of = factor_of * jnp.repeat(jnp.exp(heights), dims[axis_at] // blocks).reshape((-1,) + (1,) * (len(dims) - 1 - axis_at))
    return factor_of


def profile(count, total, limit, slope):
    weights = [(1 << 20) // math.isqrt(rank ** slope) + 1 for rank in range(2, count + 1)]
    surplus, counts = total - limit - (count - 1), [1] * (count - 1)
    while surplus > 0:
        movable = [i for i in range(count - 1) if counts[i] < limit]
        pool, remaining = sum([weights[i] for i in movable]), surplus
        for i in movable:
            extra = min(limit - counts[i], max(1, remaining * weights[i] // pool), surplus)
            counts[i] = counts[i] + extra
            surplus = surplus - extra
    return np.array([limit] + counts)


def ragged(own_key, amount, total, reach, skew):
    if amount == 2:
        one = jax.random.randint(own_key, (), max(1, total - reach), min(reach, total - 1) + 1)
        return jnp.stack([one, total - one])
    sizes = jnp.asarray(profile(amount, total, reach, skew), jnp.int32)
    pairs = (amount - 1) // 2
    donor, receiver = sizes[1:1 + 2 * pairs:2], sizes[2:2 + 2 * pairs:2]
    slack = jnp.minimum(donor - 1, reach - receiver)
    passed = jax.random.randint(jax.random.fold_in(own_key, 1), (pairs,), 0, 1 << 20) % (slack + 1)
    sizes = sizes.at[1:1 + 2 * pairs:2].set(donor - passed).at[2:2 + 2 * pairs:2].set(receiver + passed)
    return sizes[jax.random.permutation(jax.random.fold_in(own_key, 2), amount)]


def scatter_about(own_key, dims, deviation, most, split=(), kind=jnp.bfloat16):
    entries = jax.random.normal(own_key, dims, jnp.float32) * deviation
    if len(split) > 0:
        entries = block_levels(own_key, dims, split, -0.22, 0.18) * entries
    return jnp.clip(entries, min=-most, max=most).astype(kind)


def setup_inputs(seed: int = 0) -> dict:
    key_of = jax.random.split(jax.random.key(seed), 12)
    return {
        "layer_input": scatter_about(key_of[0], (NSEQ, SEQ_LEN, D), 1.0, 6.0, ((0, 8), (1, 4))),
        "first_values": scatter_about(key_of[1], (NSEQ, SEQ_LEN, (HEADS - VH) * HD), 1.0, 6.0, ((0, 8), (1, 4))),
        "segment_ids": jax.vmap(lambda own: jnp.searchsorted(jnp.cumsum(ragged(own, DOCS, SEQ_LEN, SEQ_LEN // 2, 2)), jnp.arange(SEQ_LEN), side="right"))(jax.random.split(key_of[2], NSEQ)).reshape((NSEQ, SEQ_LEN)).astype(jnp.int32),
        "pairing": draw_pairing(jax.random.fold_in(key_of[11], 71), 0),
        "norm_gains": jnp.clip(1.0 + 0.18 * jax.random.normal(key_of[4], (2, D), jnp.float32), 0.099609375, 1.8984375).astype(jnp.bfloat16),
        "norm_biases": scatter_about(key_of[5], (2, D), 0.3, 2.0, ((1, 4),)),
        "w_qkv": scatter_about(key_of[6], (D, 2 * D + VH * HD), D ** -0.5, 0.21875, ((0, 4),)),
        "w_out": scatter_about(key_of[7], (D, D), (D // 16) ** -0.5, 0.875, ((0, 4),)),
        "w_up": scatter_about(key_of[8], (D, FF), D ** -0.5, 0.21875, ((1, 4),)),
        "w_down": scatter_about(key_of[9], (FF, D), FF ** -0.5, 0.109375, ((0, 4),)),
        "cotangent": scatter_about(key_of[10], (NSEQ, SEQ_LEN, D), 1.0, 6.0, ((0, 8), (1, 4))),
    }


EPSILON = 1e-05
NEGATIVE = -1e+30
HIGHEST = lax.Precision.HIGHEST

@jax.custom_vjp
def low(v):
    return lax.optimization_barrier(v.astype(jnp.bfloat16)).astype(jnp.float32)

@jax.custom_vjp
def low_back(v):
    return v

def low_keep(v):
    return (low(v), None)

def low_pass(kept, grad):
    return (grad,)

def back_keep(v):
    return (v, None)

def back_low(kept, grad):
    return (low(grad),)
low.defvjp(low_keep, low_pass)
low_back.defvjp(back_keep, back_low)

def norm_layer(values_in, gain, bias):
    center = lax.optimization_barrier(jnp.mean(values_in, axis=-1, keepdims=True))
    centred = values_in - center
    spread = lax.optimization_barrier(jnp.mean(centred * centred, axis=-1, keepdims=True))
    return centred * lax.rsqrt(spread + EPSILON) * gain + bias

def attend(query, keys, values, query_pos, query_doc, key_pos, key_doc):
    count_rows = query.shape[0]
    query_heads = query.reshape(count_rows, HEADS, HD)
    key_heads = keys.reshape(-1, HEADS, HD)
    value_heads = values.reshape(-1, HEADS, HD)
    scores = jnp.einsum('rhd,khd->hrk', query_heads, key_heads, precision=HIGHEST) * HD ** (-0.5)
    scores = low_back(scores)
    allowed = (key_pos[None, :] <= query_pos[:, None]) & (key_doc[None, :] == query_doc[:, None])
    scores = jnp.where(allowed[None], scores, NEGATIVE)
    probs = jax.nn.softmax(scores, axis=-1)
    mixed = jnp.einsum('hrk,khd->rhd', low(probs), value_heads, precision=HIGHEST)
    return mixed.reshape(count_rows, HEADS * HD)

def layer(inputs, first, params, positions, documents):
    gains, biases, qkv_weight, out_weight, up_weight, down_weight = params
    h_one = low(norm_layer(inputs, gains[0], biases[0]))
    qkv = low(low_back(jnp.dot(h_one, qkv_weight, precision=HIGHEST)))
    query = qkv[:, :D]
    keys = qkv[:, D:2 * D]
    fresh = qkv[:, 2 * D:]
    values = jnp.concatenate([fresh, first], axis=1)
    block_rows = min(512, SEQ_LEN)
    block_count = SEQ_LEN // block_rows
    blocked = jax.checkpoint(attend)

    def one_block(items):
        query_part, pos_part, doc_part = items
        return blocked(query_part, keys, values, pos_part, doc_part, positions, documents)
    mixed = lax.map(one_block, (query.reshape(block_count, block_rows, D), positions.reshape(block_count, block_rows), documents.reshape(block_count, block_rows)))
    attn = low(low_back(mixed.reshape(SEQ_LEN, D)))
    resid = inputs + low_back(jnp.dot(attn, out_weight, precision=HIGHEST))
    h_two = low(norm_layer(resid, gains[1], biases[1]))
    upper = low_back(jnp.dot(h_two, up_weight, precision=HIGHEST))
    active = low(jax.nn.gelu(upper, approximate=True))
    return resid + low_back(jnp.dot(active, down_weight, precision=HIGHEST))

def reference(layer_input, first_values, segment_ids, pairing, norm_gains, norm_biases, w_qkv, w_out, w_up, w_down, cotangent):
    storage = jnp.arange(SEQ_LEN, dtype=jnp.int32)
    positions = (pairing[storage // BLOCK] * BLOCK + storage % BLOCK).astype(jnp.int32)
    documents = segment_ids[:, positions]
    params = (norm_gains.astype(jnp.float32), norm_biases.astype(jnp.float32), w_qkv.astype(jnp.float32), w_out.astype(jnp.float32), w_up.astype(jnp.float32), w_down.astype(jnp.float32))

    def one_sequence(totals, items):
        inputs, first, docs_row, cot_row = items

        def forward(inputs_f, first_f, params_f):
            return layer(inputs_f, first_f, params_f, positions, docs_row)
        output, backward = jax.vjp(forward, inputs.astype(jnp.float32), first.astype(jnp.float32), params)
        dinputs, dfirst, dparams = backward(cot_row.astype(jnp.float32))
        totals = jax.tree.map(lambda total, grad: total + grad, totals, dparams)
        return (totals, (output.astype(jnp.bfloat16), dinputs, dfirst))
    zeros = jax.tree.map(jnp.zeros_like, params)
    totals, (outputs, dinputs, dfirsts) = lax.scan(one_sequence, zeros, (layer_input, first_values, documents, cotangent))
    return (outputs, dinputs, dfirsts, totals[0], totals[1], totals[2], totals[3], totals[4], totals[5])
```

```python
import functools

import jax
import jax.numpy as jnp
from jax import lax
from jax.experimental import pallas as pl
from jax.experimental.pallas import tpu as pltpu
from jax.sharding import PartitionSpec as P

D = 768
HEADS = 12
HD = 64
VH = 6


EPSILON = 1e-05
NEGATIVE = -1e30


def norm_layer(values_in, gain, bias):
    center = jnp.mean(values_in, axis=-1, keepdims=True)
    centred = values_in - center
    spread = jnp.mean(centred * centred, axis=-1, keepdims=True)
    return centred * lax.rsqrt(spread + EPSILON) * gain + bias


def gelu_tanh(values_in):
    return jax.nn.gelu(values_in, approximate=True)


def block_scores(query_part, key_part, query_pos, query_doc, key_pos, key_doc):
    scale = HD ** (-0.5)
    raw = (
        jnp.einsum("rhd,khd->hrk", query_part, key_part, preferred_element_type=jnp.float32) * scale
    )
    allowed = (key_pos[None, :] <= query_pos[:, None]) & (key_doc[None, :] == query_doc[:, None])
    return (raw, allowed[None])


def wide_body(
    layer_input,
    first_values,
    segment_ids,
    pairing,
    norm_gains,
    norm_biases,
    w_qkv,
    w_out,
    w_up,
    w_down,
    cotangent,
):
    scale = HD ** (-0.5)
    ctx_index = lax.axis_index("ctx")
    local_rows = layer_input.shape[1]
    half_rows = local_rows // 2
    seq_length = local_rows * lax.axis_size("ctx")
    key_block = min(512, seq_length)
    key_count = seq_length // key_block
    offsets = jnp.arange(half_rows, dtype=jnp.int32)
    all_pos = (pairing[:, None] * half_rows + offsets[None, :]).reshape(seq_length)
    own_blocks = lax.dynamic_slice_in_dim(pairing, 2 * ctx_index, 2)
    own_pos = (own_blocks[:, None] * half_rows + offsets[None, :]).reshape(local_rows)
    doc_row = segment_ids[0]
    all_doc = jnp.take(doc_row, all_pos)
    own_doc = jnp.take(doc_row, own_pos)
    gathered = (
        lax.all_gather(norm_gains, "fsdp", axis=1, tiled=True),
        lax.all_gather(norm_biases, "fsdp", axis=1, tiled=True),
        lax.all_gather(w_qkv, "fsdp", axis=0, tiled=True),
        lax.all_gather(w_out, "fsdp", axis=0, tiled=True),
        lax.all_gather(w_up, "fsdp", axis=1, tiled=True),
        lax.all_gather(w_down, "fsdp", axis=0, tiled=True),
    )
    gains_all, biases_all, qkv_full, out_full, up_full, down_full = gathered
    gains = gains_all.astype(jnp.float32)
    biases = biases_all.astype(jnp.float32)
    inputs = layer_input[0].astype(jnp.float32)
    normed_one, norm_one_back = jax.vjp(norm_layer, inputs, gains[0], biases[0])
    h_one = normed_one.astype(jnp.bfloat16)
    qkv_low = jnp.dot(h_one, qkv_full, preferred_element_type=jnp.float32).astype(jnp.bfloat16)
    query_low = qkv_low[:, :D]
    key_low = qkv_low[:, D : 2 * D]
    fresh_low = qkv_low[:, 2 * D :]
    values_low = jnp.concatenate([fresh_low, first_values[0]], axis=1)
    keys_all, values_all = (
        lax.all_gather(key_low, "ctx", axis=0, tiled=True),
        lax.all_gather(values_low, "ctx", axis=0, tiled=True),
    )
    query_heads = query_low.reshape(local_rows, HEADS, HD)
    key_blocks = keys_all.reshape(key_count, key_block, HEADS, HD)
    value_blocks = values_all.reshape(key_count, key_block, HEADS, HD)
    pos_blocks = all_pos.reshape(key_count, key_block)
    doc_blocks = all_doc.reshape(key_count, key_block)

    def stats_step(carry, block):
        running_top, running_total = carry
        key_part, key_pos, key_doc = block
        raw, allowed = block_scores(query_heads, key_part, own_pos, own_doc, key_pos, key_doc)
        masked = jnp.where(allowed, raw, NEGATIVE)
        new_top = jnp.maximum(running_top, jnp.max(masked, axis=-1))
        terms = jnp.where(allowed, jnp.exp(raw - new_top[..., None]), 0.0)
        running_total = running_total * jnp.exp(running_top - new_top) + jnp.sum(terms, axis=-1)
        return ((new_top, running_total), None)

    start_top = jnp.full((HEADS, local_rows), NEGATIVE, jnp.float32)
    start_total = jnp.zeros((HEADS, local_rows), jnp.float32)
    (final_top, final_total), _ = lax.scan(
        stats_step, (start_top, start_total), (key_blocks, pos_blocks, doc_blocks)
    )
    log_total = final_top + jnp.log(final_total)

    def mix_step(accum, block):
        key_part, value_part, key_pos, key_doc = block
        raw, allowed = block_scores(query_heads, key_part, own_pos, own_doc, key_pos, key_doc)
        probs = jnp.where(allowed, jnp.exp(raw - log_total[..., None]), 0.0).astype(jnp.bfloat16)
        return (
            accum
            + jnp.einsum("hrk,khd->rhd", probs, value_part, preferred_element_type=jnp.float32),
            None,
        )

    mixed, _ = lax.scan(
        mix_step,
        jnp.zeros((local_rows, HEADS, HD), jnp.float32),
        (key_blocks, value_blocks, pos_blocks, doc_blocks),
    )
    attn_low = mixed.reshape(local_rows, D).astype(jnp.bfloat16)
    resid = inputs + jnp.dot(attn_low, out_full, preferred_element_type=jnp.float32)
    normed_two, norm_two_back = jax.vjp(norm_layer, resid, gains[1], biases[1])
    h_two = normed_two.astype(jnp.bfloat16)
    upper = jnp.dot(h_two, up_full, preferred_element_type=jnp.float32)
    active, gelu_back = jax.vjp(gelu_tanh, upper)
    active_low = active.astype(jnp.bfloat16)
    layer_out = (resid + jnp.dot(active_low, down_full, preferred_element_type=jnp.float32)).astype(
        jnp.bfloat16
    )
    regathered = (
        lax.all_gather(norm_gains, "fsdp", axis=1, tiled=True),
        lax.all_gather(norm_biases, "fsdp", axis=1, tiled=True),
        lax.all_gather(w_qkv, "fsdp", axis=0, tiled=True),
        lax.all_gather(w_out, "fsdp", axis=0, tiled=True),
        lax.all_gather(w_up, "fsdp", axis=1, tiled=True),
        lax.all_gather(w_down, "fsdp", axis=0, tiled=True),
    )
    qkv_back = regathered[2]
    out_back = regathered[3]
    up_back = regathered[4]
    down_back = regathered[5]
    cot_low = cotangent[0]
    cot_full = cot_low.astype(jnp.float32)
    down_grad = jnp.dot(active_low.T, cot_low, preferred_element_type=jnp.float32)
    dactive = jnp.dot(cot_low, down_back.T, preferred_element_type=jnp.float32)
    dupper_low = gelu_back(dactive)[0].astype(jnp.bfloat16)
    up_grad = jnp.dot(h_two.T, dupper_low, preferred_element_type=jnp.float32)
    dh_two = jnp.dot(dupper_low, up_back.T, preferred_element_type=jnp.float32)
    dresid_norm, gain_two_grad, bias_two_grad = norm_two_back(dh_two)
    dresid = cot_full + dresid_norm
    dbranch_low = dresid.astype(jnp.bfloat16)
    out_grad = jnp.dot(attn_low.T, dbranch_low, preferred_element_type=jnp.float32)
    dmixed_low = jnp.dot(dbranch_low, out_back.T, preferred_element_type=jnp.float32).astype(
        jnp.bfloat16
    )
    dmixed_heads = dmixed_low.reshape(local_rows, HEADS, HD)
    row_terms = jnp.sum(dmixed_heads.astype(jnp.float32) * mixed, axis=-1).T

    def grad_step(accum, block):
        key_part, value_part, key_pos, key_doc = block
        raw, allowed = block_scores(query_heads, key_part, own_pos, own_doc, key_pos, key_doc)
        probs = jnp.where(allowed, jnp.exp(raw - log_total[..., None]), 0.0)
        dprobs = jnp.einsum(
            "rhd,khd->hrk", dmixed_heads, value_part, preferred_element_type=jnp.float32
        )
        dscore_low = (probs * (dprobs - row_terms[..., None])).astype(jnp.bfloat16)
        accum = accum + jnp.einsum(
            "hrk,khd->rhd", dscore_low, key_part, preferred_element_type=jnp.float32
        )
        dkey_part = jnp.einsum(
            "hrk,rhd->khd", dscore_low, query_heads, preferred_element_type=jnp.float32
        )
        dvalue_part = jnp.einsum(
            "hrk,rhd->khd",
            probs.astype(jnp.bfloat16),
            dmixed_heads,
            preferred_element_type=jnp.float32,
        )
        return (accum, (dkey_part, dvalue_part))

    dquery_sum, (dkey_parts, dvalue_parts) = lax.scan(
        grad_step,
        jnp.zeros((local_rows, HEADS, HD), jnp.float32),
        (key_blocks, value_blocks, pos_blocks, doc_blocks),
    )
    dkeys_all = dkey_parts.reshape(seq_length, D) * scale
    dvalues_all = dvalue_parts.reshape(seq_length, D)
    own_dkeys, own_dvalues = (
        lax.psum_scatter(
            dkeys_all.astype(jnp.bfloat16), "ctx", scatter_dimension=0, tiled=True
        ).astype(jnp.float32),
        lax.psum_scatter(
            dvalues_all.astype(jnp.bfloat16), "ctx", scatter_dimension=0, tiled=True
        ).astype(jnp.float32),
    )
    dquery = dquery_sum.reshape(local_rows, D) * scale
    fresh_width = VH * HD
    first_grad = own_dvalues[:, fresh_width:]
    dqkv_low = jnp.concatenate(
        [
            dquery.astype(jnp.bfloat16),
            own_dkeys.astype(jnp.bfloat16),
            own_dvalues[:, :fresh_width].astype(jnp.bfloat16),
        ],
        axis=1,
    )
    qkv_grad = jnp.dot(h_one.T, dqkv_low, preferred_element_type=jnp.float32)
    dh_one = jnp.dot(dqkv_low, qkv_back.T, preferred_element_type=jnp.float32)
    dinput_norm, gain_one_grad, bias_one_grad = norm_one_back(dh_one)
    input_grad = dresid + dinput_norm
    gain_grads = jnp.stack([gain_one_grad, gain_two_grad])
    bias_grads = jnp.stack([bias_one_grad, bias_two_grad])
    shares = (
        lax.psum_scatter(
            gain_grads.astype(jnp.bfloat16), "fsdp", scatter_dimension=1, tiled=True
        ).astype(jnp.float32),
        lax.psum_scatter(
            bias_grads.astype(jnp.bfloat16), "fsdp", scatter_dimension=1, tiled=True
        ).astype(jnp.float32),
        lax.psum_scatter(
            qkv_grad.astype(jnp.bfloat16), "fsdp", scatter_dimension=0, tiled=True
        ).astype(jnp.float32),
        lax.psum_scatter(
            out_grad.astype(jnp.bfloat16), "fsdp", scatter_dimension=0, tiled=True
        ).astype(jnp.float32),
        lax.psum_scatter(
            up_grad.astype(jnp.bfloat16), "fsdp", scatter_dimension=1, tiled=True
        ).astype(jnp.float32),
        lax.psum_scatter(
            down_grad.astype(jnp.bfloat16), "fsdp", scatter_dimension=0, tiled=True
        ).astype(jnp.float32),
    )
    summed = (
        lax.psum(shares[0].astype(jnp.bfloat16), ("dp", "ctx")).astype(jnp.float32),
        lax.psum(shares[1].astype(jnp.bfloat16), ("dp", "ctx")).astype(jnp.float32),
        lax.psum(shares[2].astype(jnp.bfloat16), ("dp", "ctx")).astype(jnp.float32),
        lax.psum(shares[3].astype(jnp.bfloat16), ("dp", "ctx")).astype(jnp.float32),
        lax.psum(shares[4].astype(jnp.bfloat16), ("dp", "ctx")).astype(jnp.float32),
        lax.psum(shares[5].astype(jnp.bfloat16), ("dp", "ctx")).astype(jnp.float32),
    )
    return (
        layer_out[None],
        input_grad[None],
        first_grad[None],
        summed[0],
        summed[1],
        summed[2],
        summed[3],
        summed[4],
        summed[5],
    )


BLK = 256
GW = 3 * HD
LOG2E = 1.4426950408889634


def block_rows(index):
    return pl.ds(pl.multiple_of(index, BLK), BLK)


def attn_fwd_kernel(roff, jmin, start_ref, qkv_ref, o_ref, ot_ref, lse_ref, vt_ref, m_ref, l_ref, acc_ref):
    blocks = qkv_ref.shape[0] // BLK
    factor = HD ** (-0.5) * LOG2E
    iota_k = lax.broadcasted_iota(jnp.int32, (BLK, BLK), 0)
    iota_q = lax.broadcasted_iota(jnp.int32, (BLK, BLK), 1)

    def flip(p, carry):
        rows = block_rows(roff[p])
        for h in range(3):
            vt_ref[h, p] = qkv_ref[rows, 2 * GW + h * HD : 2 * GW + (h + 1) * HD].T
        return carry

    lax.fori_loop(0, blocks, flip, 0)

    def query_block(i, carry):
        rows = block_rows(roff[i])
        start = start_ref[pl.ds(i, 1), :]
        qts = [qkv_ref[rows, h * HD : (h + 1) * HD].T for h in range(3)]
        for h in range(3):
            m_ref[h] = jnp.full((1, BLK), NEGATIVE, jnp.float32)
            l_ref[h] = jnp.zeros((1, BLK), jnp.float32)
            acc_ref[h] = jnp.zeros((HD, BLK), jnp.float32)

        def step(j, causal):
            krows = block_rows(roff[j])
            allowed = iota_k + j * BLK >= start
            if causal:
                allowed = allowed & (iota_k <= iota_q)
            for h in range(3):
                kh = qkv_ref[krows, GW + h * HD : GW + (h + 1) * HD]
                st = jnp.dot(kh, qts[h], preferred_element_type=jnp.float32) * factor
                st = jnp.where(allowed, st, NEGATIVE)
                m_old = m_ref[h]
                m_new = jnp.maximum(m_old, jnp.max(st, axis=0, keepdims=True))
                pt = jnp.exp2(st - m_new)
                alpha = jnp.exp2(m_old - m_new)
                m_ref[h] = m_new
                l_ref[h] = l_ref[h] * alpha + jnp.sum(pt, axis=0, keepdims=True)
                acc_ref[h] = acc_ref[h] * alpha + jnp.dot(
                    vt_ref[h, j], pt.astype(jnp.bfloat16), preferred_element_type=jnp.float32
                )

        def off_diagonal(j, c):
            step(j, False)
            return c

        lax.fori_loop(jmin[i], i, off_diagonal, 0)
        step(i, True)
        for h in range(3):
            total = l_ref[h]
            ot = acc_ref[h] / total
            ot_ref[h, i] = ot
            lse_ref[h, pl.ds(i, 1), :] = m_ref[h] + jnp.log2(total)
            o_ref[rows, h * HD : (h + 1) * HD] = ot.T.astype(jnp.bfloat16)
        return carry

    lax.fori_loop(0, blocks, query_block, 0)


def attn_bwd_kernel(roff, jmin, start_ref, qkv_ref, do_ref, ot_ref, lse_ref, out_ref, kt_ref, dqt_ref, dk_ref, dv_ref):
    blocks = qkv_ref.shape[0] // BLK
    scale = HD ** (-0.5)
    factor = scale * LOG2E
    iota_k = lax.broadcasted_iota(jnp.int32, (BLK, BLK), 0)
    iota_q = lax.broadcasted_iota(jnp.int32, (BLK, BLK), 1)

    def prepare(p, carry):
        rows = block_rows(roff[p])
        for h in range(3):
            kt_ref[h, p] = qkv_ref[rows, GW + h * HD : GW + (h + 1) * HD].T
            dk_ref[h, p] = jnp.zeros((BLK, HD), jnp.float32)
            dv_ref[h, p] = jnp.zeros((BLK, HD), jnp.float32)
        return carry

    lax.fori_loop(0, blocks, prepare, 0)

    def query_block(i, carry):
        rows = block_rows(roff[i])
        start = start_ref[pl.ds(i, 1), :]
        qs = [qkv_ref[rows, h * HD : (h + 1) * HD] for h in range(3)]
        qts = [q.T for q in qs]
        dos = [do_ref[rows, h * HD : (h + 1) * HD] for h in range(3)]
        dots = [d.T for d in dos]
        lses = [lse_ref[h, pl.ds(i, 1), :] for h in range(3)]
        deltas = [
            jnp.sum(dots[h].astype(jnp.float32) * ot_ref[h, i], axis=0, keepdims=True)
            for h in range(3)
        ]
        for h in range(3):
            dqt_ref[h] = jnp.zeros((HD, BLK), jnp.float32)

        def step(j, causal):
            krows = block_rows(roff[j])
            allowed = iota_k + j * BLK >= start
            if causal:
                allowed = allowed & (iota_k <= iota_q)
            for h in range(3):
                kh = qkv_ref[krows, GW + h * HD : GW + (h + 1) * HD]
                vh = qkv_ref[krows, 2 * GW + h * HD : 2 * GW + (h + 1) * HD]
                st = jnp.dot(kh, qts[h], preferred_element_type=jnp.float32)
                dpt = jnp.dot(vh, dots[h], preferred_element_type=jnp.float32)
                pt = jnp.where(allowed, jnp.exp2(st * factor - lses[h]), 0.0)
                dst = (pt * (dpt - deltas[h])).astype(jnp.bfloat16)
                dv_ref[h, j] += jnp.dot(
                    pt.astype(jnp.bfloat16), dos[h], preferred_element_type=jnp.float32
                )
                dk_ref[h, j] += jnp.dot(dst, qs[h], preferred_element_type=jnp.float32)
                dqt_ref[h] += jnp.dot(kt_ref[h, j], dst, preferred_element_type=jnp.float32)

        def off_diagonal(j, c):
            step(j, False)
            return c

        lax.fori_loop(jmin[i], i, off_diagonal, 0)
        step(i, True)
        for h in range(3):
            out_ref[rows, h * HD : (h + 1) * HD] = (dqt_ref[h] * scale).T.astype(jnp.bfloat16)
        return carry

    lax.fori_loop(0, blocks, query_block, 0)

    def finish(p, carry):
        rows = block_rows(roff[p])
        for h in range(3):
            out_ref[rows, GW + h * HD : GW + (h + 1) * HD] = (dk_ref[h, p] * scale).astype(
                jnp.bfloat16
            )
            out_ref[rows, 2 * GW + h * HD : 2 * GW + (h + 1) * HD] = dv_ref[h, p].astype(
                jnp.bfloat16
            )
        return carry

    lax.fori_loop(0, blocks, finish, 0)


SMEM_SPEC = pl.BlockSpec(memory_space=pltpu.SMEM)
VMEM_SPEC = pl.BlockSpec(memory_space=pltpu.VMEM)


def attn_forward(roff, jmin, starts, qkv):
    length = qkv.shape[0]
    blocks = length // BLK
    return pl.pallas_call(
        attn_fwd_kernel,
        name="attn_forward",
        out_shape=(
            jax.ShapeDtypeStruct((length, GW), jnp.bfloat16),
            jax.ShapeDtypeStruct((3, blocks, HD, BLK), jnp.float32),
            jax.ShapeDtypeStruct((3, blocks, BLK), jnp.float32),
        ),
        in_specs=[SMEM_SPEC, SMEM_SPEC, VMEM_SPEC, VMEM_SPEC],
        out_specs=(VMEM_SPEC, VMEM_SPEC, VMEM_SPEC),
        scratch_shapes=[
            pltpu.VMEM((3, blocks, HD, BLK), jnp.bfloat16),
            pltpu.VMEM((3, 1, BLK), jnp.float32),
            pltpu.VMEM((3, 1, BLK), jnp.float32),
            pltpu.VMEM((3, HD, BLK), jnp.float32),
        ],
    )(roff, jmin, starts, qkv)


def attn_backward(roff, jmin, starts, qkv, dout, ot, lse):
    length = qkv.shape[0]
    blocks = length // BLK
    return pl.pallas_call(
        attn_bwd_kernel,
        name="attn_backward",
        out_shape=jax.ShapeDtypeStruct((length, 3 * GW), jnp.bfloat16),
        in_specs=[SMEM_SPEC, SMEM_SPEC] + [VMEM_SPEC] * 5,
        out_specs=VMEM_SPEC,
        scratch_shapes=[
            pltpu.VMEM((3, blocks, HD, BLK), jnp.bfloat16),
            pltpu.VMEM((3, HD, BLK), jnp.float32),
            pltpu.VMEM((3, blocks, BLK, HD), jnp.float32),
            pltpu.VMEM((3, blocks, BLK, HD), jnp.float32),
        ],
    )(roff, jmin, starts, qkv, dout, ot, lse)


def shift_ctx(value, shift):
    return lax.ppermute(value, "ctx", [(i, (i + shift) % 4) for i in range(4)])


def swap_core(value):
    return lax.ppermute(value, "fsdp", [(i, i ^ 1) for i in range(4)])


def swap_x(value):
    return lax.ppermute(value, "fsdp", [(i, i ^ 2) for i in range(4)])


def swap_dp(value):
    return lax.ppermute(value, "dp", [(0, 1), (1, 0)])


def gather_fsdp(value):
    index = lax.axis_index("fsdp")
    other = swap_x(value)
    pair = jnp.stack([value, other])
    far = swap_core(pair)
    stacked = jnp.concatenate([pair, far])
    parts = [
        lax.dynamic_index_in_dim(stacked, order_of(index, wanted), 0, keepdims=False)
        for wanted in range(4)
    ]
    return jnp.concatenate(parts, axis=0)


def order_of(index, wanted):
    apart = jnp.bitwise_xor(index, wanted)
    return (apart >> 1) + 2 * (apart & 1)


def dot32(a, b):
    return jnp.dot(a, b, preferred_element_type=jnp.float32)


def dot_nt(a, b):
    return lax.dot_general(a, b, (((1,), (1,)), ((), ())), preferred_element_type=jnp.float32)


def dot_tn(a, b):
    return lax.dot_general(a, b, (((0,), (0,)), ((), ())), preferred_element_type=jnp.float32)


def normalize(values_in):
    center = jnp.mean(values_in, axis=-1, keepdims=True)
    centred = values_in - center
    spread = lax.rsqrt(jnp.mean(centred * centred, axis=-1, keepdims=True) + EPSILON)
    return centred * spread, spread


def norm_back(grad, unit, spread, gain):
    scaled = grad * gain
    return spread * (
        scaled
        - jnp.mean(scaled, axis=-1, keepdims=True)
        - unit * jnp.mean(scaled * unit, axis=-1, keepdims=True)
    )


GROUP_OF = (0, 2, 3, 1)


def grouped_body(
    layer_input,
    first_values,
    segment_ids,
    pairing,
    norm_gains,
    norm_biases,
    w_qkv,
    w_out,
    w_up,
    w_down,
    cotangent,
):
    ctx = lax.axis_index("ctx")
    fsdp = lax.axis_index("fsdp")
    core = fsdp % 2
    rows = layer_input.shape[1]
    length = rows * 4
    blocks = length // BLK
    group_table = jnp.array(GROUP_OF, jnp.int32)
    group_at = [group_table[(ctx + s) % 4] for s in range(4)]
    own_group = group_at[0]

    doc_row = segment_ids[0]
    starts = jnp.sum(
        (doc_row[None, :] < doc_row[:, None]).astype(jnp.int32), axis=1, dtype=jnp.int32
    ).reshape(blocks, BLK)
    firsts, lasts = doc_row[::BLK], doc_row[BLK - 1 :: BLK]
    jmin = jnp.sum((lasts[None, :] < firsts[:, None]).astype(jnp.int32), axis=1, dtype=jnp.int32)
    block_ids = jnp.arange(blocks, dtype=jnp.int32)
    held_at = jnp.sum(
        jnp.where(pairing[None, :] == block_ids[:, None], block_ids[None, :], 0), axis=1, dtype=jnp.int32
    )
    roff = ((ctx - held_at // 2) % 4) * rows + (held_at % 2) * BLK

    first = first_values[0]
    lower, upper_half = first[:, :GW], first[:, GW:]
    first_parts = [jnp.where(ctx == 1, lower, upper_half)]
    for s in range(1, 4):
        message = jnp.where((ctx + s) % 4 == 1, lower, upper_half)
        pairs = [(i, (i + s) % 4) for i in range(4) if (i + s) % 4 in (1, 2)]
        first_parts.append(lax.ppermute(message, "ctx", pairs))
    reuses = (ctx == 1) | (ctx == 2)

    norms = jnp.concatenate([norm_gains, norm_biases], axis=0)
    norm_rows = jnp.zeros((192, 128), jnp.bfloat16).at[:, :4].set(norms.T)
    qkv_shard = jnp.concatenate([w_qkv, norm_rows], axis=1)
    qkv_all = gather_fsdp(qkv_shard)
    qkv_full = qkv_all[:, : w_qkv.shape[1]]
    norm_cols = qkv_all[:, w_qkv.shape[1] : w_qkv.shape[1] + 4].astype(jnp.float32)
    gain1_col, bias1_col = norm_cols[:, 0:1], norm_cols[:, 2:3]
    norm_lines = norm_cols.T
    gain1, gain2, bias1, bias2 = [norm_lines[k][None, :] for k in range(4)]
    out_full = gather_fsdp(w_out)
    up_half = jnp.concatenate([w_up, swap_x(w_up)], axis=1)
    down_half = jnp.concatenate([w_down, swap_x(w_down)], axis=0)
    fresh_width = VH * HD
    grouped = []
    for g in range(4):
        wv = (
            qkv_full[:, 2 * D + g * GW : 2 * D + (g + 1) * GW]
            if (g + 1) * GW <= fresh_width
            else jnp.zeros((D, GW), jnp.bfloat16)
        )
        grouped.append(
            jnp.concatenate(
                [qkv_full[:, g * GW : (g + 1) * GW], qkv_full[:, D + g * GW : D + (g + 1) * GW], wv],
                axis=1,
            )
        )
    grouped = jnp.stack(grouped)
    w_groups = [lax.dynamic_index_in_dim(grouped, group_at[s], 0, keepdims=False) for s in range(4)]
    w_own = w_groups[0]
    w_turned = jnp.concatenate(w_groups, axis=1)
    out_turned = jnp.concatenate(
        [lax.dynamic_slice_in_dim(out_full, group_at[s] * GW, GW, axis=0) for s in range(4)], axis=0
    )

    chunk = layer_input[0]
    half = rows // 2
    parts = [chunk[:half], chunk[half:]]
    slots = [chunk]
    for s in range(3):
        parts = [shift_ctx(part, 1) for part in parts]
        slots.append(jnp.concatenate(parts, axis=0))
    unit_slots, qkv_slots = [], []
    for s in range(4):
        unit, spread = normalize(slots[s].astype(jnp.float32))
        if s == 0:
            own_unit, own_spread = unit, spread
        h_one = (unit * gain1 + bias1).astype(jnp.bfloat16)
        part = dot32(h_one, w_own).astype(jnp.bfloat16)
        value = jnp.where(reuses, first_parts[s], part[:, 2 * GW :])
        qkv_slots.append(jnp.concatenate([part[:, : 2 * GW], value], axis=1))
        unit_slots.append(unit.astype(jnp.bfloat16))
    qkv_heads = jnp.concatenate(qkv_slots, axis=0)
    unit_all = jnp.concatenate(unit_slots, axis=0)

    cot_own = cotangent[0]
    cot_both = jnp.concatenate([cot_own, swap_core(cot_own)], axis=0)
    dactive = dot_nt(cot_both, down_half).astype(jnp.bfloat16)

    mixed, mixed_t, lse = attn_forward(roff, jmin, starts, qkv_heads)
    pieces = [mixed[:rows]] + [
        shift_ctx(mixed[s * rows : (s + 1) * rows], -s) for s in range(1, 4)
    ]
    attn_low = jnp.concatenate(pieces, axis=1)
    resid = chunk.astype(jnp.float32) + dot32(attn_low, out_turned)
    unit_two, spread_two = normalize(resid)
    h_two = (unit_two * gain2 + bias2).astype(jnp.bfloat16)
    h_both = jnp.concatenate([h_two, swap_core(h_two)], axis=0)

    upper = dot32(h_both, up_half)
    root = 0.7978845608028654
    squared = upper * upper
    tanned = jnp.tanh(root * upper * (1.0 + 0.044715 * squared))
    active_low = (0.5 * upper * (1.0 + tanned)).astype(jnp.bfloat16)
    slope = 0.5 * (1.0 + tanned) + 0.5 * upper * (1.0 - tanned * tanned) * root * (
        1.0 + 3.0 * 0.044715 * squared
    )
    dupper_low = (dactive.astype(jnp.float32) * slope).astype(jnp.bfloat16)

    dh_both = dot_nt(dupper_low, up_half)
    dh_two = dh_both[:rows] + swap_core(dh_both[rows:].astype(jnp.bfloat16)).astype(jnp.float32)
    gain_two_grad = jnp.sum(dh_two * unit_two, axis=0)
    bias_two_grad = jnp.sum(dh_two, axis=0)
    dresid = cot_own.astype(jnp.float32) + norm_back(dh_two, unit_two, spread_two, gain2)
    dbranch_low = dresid.astype(jnp.bfloat16)
    dmixed = dot_nt(dbranch_low, out_turned).astype(jnp.bfloat16)
    dmixed_slots = [dmixed[:, :GW]] + [
        shift_ctx(dmixed[:, s * GW : (s + 1) * GW], s) for s in range(1, 4)
    ]
    dmixed_all = jnp.concatenate(dmixed_slots, axis=0)

    out_both = dot32(active_low, down_half)
    layer_out = (
        resid + out_both[:rows] + swap_core(out_both[rows:].astype(jnp.bfloat16)).astype(jnp.float32)
    ).astype(jnp.bfloat16)

    down_grad = dot_tn(active_low, cot_both)
    up_grad = dot_tn(h_both, dupper_low)
    width = w_up.shape[1]
    down_sum = down_grad[:width] + swap_x(down_grad[width:].astype(jnp.bfloat16)).astype(jnp.float32)
    up_sum = up_grad[:, :width] + swap_x(up_grad[:, width:].astype(jnp.bfloat16)).astype(jnp.float32)
    out_turned_grad = dot_tn(attn_low, dbranch_low)
    out_parts = out_turned_grad.reshape(4, GW, D)
    place = jnp.array([GROUP_OF.index(g) for g in range(4)], jnp.int32)
    out_rows = [
        lax.dynamic_index_in_dim(out_parts, (place[g] - ctx) % 4, 0, keepdims=False) for g in range(4)
    ]
    shares = jnp.stack(out_rows)
    out_sum = reduce_fsdp(shares, fsdp)
    down_low, up_low, out_low = lax.psum(
        (down_sum.astype(jnp.bfloat16), up_sum.astype(jnp.bfloat16), out_sum.astype(jnp.bfloat16)),
        ("dp", "ctx"),
    )

    dqkv = attn_backward(roff, jmin, starts, qkv_heads, dmixed_all, mixed_t, lse)
    back = [dqkv[:rows]] + [shift_ctx(dqkv[s * rows : (s + 1) * rows], -s) for s in range(1, 4)]

    product = dot_tn(unit_all, dqkv)
    sums = jnp.sum(dqkv.astype(jnp.float32), axis=0, keepdims=True)
    w_own32 = w_own.astype(jnp.float32)
    gain_one_col = jnp.sum(w_own32 * product, axis=1, keepdims=True)
    bias_one_col = jnp.sum(w_own32 * sums, axis=1, keepdims=True)
    qkv_part = gain1_col * product + bias1_col * sums
    extra = jnp.concatenate(
        [gain_one_col, gain_two_grad[:, None], bias_one_col, bias_two_grad[:, None], jnp.zeros((D, 60), jnp.float32)],
        axis=1,
    )
    share = jnp.concatenate([qkv_part, extra], axis=1).reshape(4, D // 4, 3 * GW + 64)
    share = reduce_fsdp(share, fsdp)
    share_low = share.astype(jnp.bfloat16)
    share = share + swap_dp(share_low).astype(jnp.float32)
    share_low = share.astype(jnp.bfloat16)
    others = jnp.stack([share_low] + [shift_ctx(share_low, -s) for s in range(1, 4)])
    by_group = [
        lax.dynamic_index_in_dim(others, (place[g] - ctx) % 4, 0, keepdims=False).astype(jnp.float32)
        for g in range(4)
    ]
    qkv_grad = jnp.concatenate(
        [b[:, :GW] for b in by_group]
        + [b[:, GW : 2 * GW] for b in by_group]
        + [by_group[g][:, 2 * GW : 3 * GW] for g in range(2)],
        axis=1,
    )
    tails = sum(b[:, 3 * GW : 3 * GW + 4] for b in by_group)
    norm_grads = tails.T
    gains_grad, biases_grad = norm_grads[:2], norm_grads[2:4]

    back_all = jnp.concatenate(back, axis=1)
    dh_one = dot_nt(back_all, w_turned)
    input_grad = dresid + norm_back(dh_one, own_unit, own_spread, gain1)
    value_parts = jnp.stack([b[:, 2 * GW :] for b in back])
    first_grad = jnp.concatenate(
        [
            lax.dynamic_index_in_dim(value_parts, (place[g] - ctx) % 4, 0, keepdims=False)
            for g in (2, 3)
        ],
        axis=1,
    ).astype(jnp.float32)

    return (
        layer_out[None],
        input_grad[None],
        first_grad[None],
        gains_grad,
        biases_grad,
        qkv_grad,
        out_low.astype(jnp.float32),
        up_low.astype(jnp.float32),
        down_low.astype(jnp.float32),
    )


def reduce_fsdp(shares, fsdp):
    turned = shares.reshape((2, 2) + shares.shape[1:])
    core = fsdp % 2
    x = fsdp // 2
    keep = lax.dynamic_index_in_dim(turned, core, 1, keepdims=False)
    give = lax.dynamic_index_in_dim(turned, 1 - core, 1, keepdims=False)
    pair = keep + swap_core(give.astype(jnp.bfloat16)).astype(jnp.float32)
    mine = lax.dynamic_index_in_dim(pair, x, 0, keepdims=False)
    other = lax.dynamic_index_in_dim(pair, 1 - x, 0, keepdims=False)
    return mine + swap_x(other.astype(jnp.bfloat16)).astype(jnp.float32)


def solution(mesh):
    sizes = dict(mesh.shape)
    small = sizes["dp"] == 2 and sizes["ctx"] == 4 and sizes["fsdp"] == 4
    chosen = grouped_body if small else wide_body
    in_specs = (
        P(("dp", "fsdp"), "ctx", None),
        P(("dp", "fsdp"), "ctx", None),
        P(("dp", "fsdp"), None),
        P(),
        P(None, "fsdp"),
        P(None, "fsdp"),
        P("fsdp", None),
        P("fsdp", None),
        P(None, "fsdp"),
        P("fsdp", None),
        P(("dp", "fsdp"), "ctx", None),
    )
    out_specs = (
        P(("dp", "fsdp"), "ctx", None),
        P(("dp", "fsdp"), "ctx", None),
        P(("dp", "fsdp"), "ctx", None),
        P(None, "fsdp"),
        P(None, "fsdp"),
        P("fsdp", None),
        P("fsdp", None),
        P(None, "fsdp"),
        P("fsdp", None),
    )
    return jax.shard_map(chosen, mesh=mesh, in_specs=in_specs, out_specs=out_specs, check_vma=False)
```

```python
import functools

import jax
import jax.numpy as jnp
from jax import lax
from jax.experimental import pallas as pl
from jax.experimental.pallas import tpu as pltpu
from jax.sharding import PartitionSpec as P

D = 768
HEADS = 12
HD = 64
VH = 6


EPSILON = 1e-05
NEGATIVE = -1e30


def norm_layer(values_in, gain, bias):
    center = jnp.mean(values_in, axis=-1, keepdims=True)
    centred = values_in - center
    spread = jnp.mean(centred * centred, axis=-1, keepdims=True)
    return centred * lax.rsqrt(spread + EPSILON) * gain + bias


def gelu_tanh(values_in):
    return jax.nn.gelu(values_in, approximate=True)


def block_scores(query_part, key_part, query_pos, query_doc, key_pos, key_doc):
    scale = HD ** (-0.5)
    raw = (
        jnp.einsum("rhd,khd->hrk", query_part, key_part, preferred_element_type=jnp.float32) * scale
    )
    allowed = (key_pos[None, :] <= query_pos[:, None]) & (key_doc[None, :] == query_doc[:, None])
    return (raw, allowed[None])


def wide_body(
    layer_input,
    first_values,
    segment_ids,
    pairing,
    norm_gains,
    norm_biases,
    w_qkv,
    w_out,
    w_up,
    w_down,
    cotangent,
):
    scale = HD ** (-0.5)
    ctx_index = lax.axis_index("ctx")
    local_rows = layer_input.shape[1]
    half_rows = local_rows // 2
    seq_length = local_rows * lax.axis_size("ctx")
    key_block = min(512, seq_length)
    key_count = seq_length // key_block
    offsets = jnp.arange(half_rows, dtype=jnp.int32)
    all_pos = (pairing[:, None] * half_rows + offsets[None, :]).reshape(seq_length)
    own_blocks = lax.dynamic_slice_in_dim(pairing, 2 * ctx_index, 2)
    own_pos = (own_blocks[:, None] * half_rows + offsets[None, :]).reshape(local_rows)
    doc_row = segment_ids[0]
    all_doc = jnp.take(doc_row, all_pos)
    own_doc = jnp.take(doc_row, own_pos)
    gathered = (
        lax.all_gather(norm_gains, "fsdp", axis=1, tiled=True),
        lax.all_gather(norm_biases, "fsdp", axis=1, tiled=True),
        lax.all_gather(w_qkv, "fsdp", axis=0, tiled=True),
        lax.all_gather(w_out, "fsdp", axis=0, tiled=True),
        lax.all_gather(w_up, "fsdp", axis=1, tiled=True),
        lax.all_gather(w_down, "fsdp", axis=0, tiled=True),
    )
    gains_all, biases_all, qkv_full, out_full, up_full, down_full = gathered
    gains = gains_all.astype(jnp.float32)
    biases = biases_all.astype(jnp.float32)
    inputs = layer_input[0].astype(jnp.float32)
    normed_one, norm_one_back = jax.vjp(norm_layer, inputs, gains[0], biases[0])
    h_one = normed_one.astype(jnp.bfloat16)
    qkv_low = jnp.dot(h_one, qkv_full, preferred_element_type=jnp.float32).astype(jnp.bfloat16)
    query_low = qkv_low[:, :D]
    key_low = qkv_low[:, D : 2 * D]
    fresh_low = qkv_low[:, 2 * D :]
    values_low = jnp.concatenate([fresh_low, first_values[0]], axis=1)
    keys_all, values_all = (
        lax.all_gather(key_low, "ctx", axis=0, tiled=True),
        lax.all_gather(values_low, "ctx", axis=0, tiled=True),
    )
    query_heads = query_low.reshape(local_rows, HEADS, HD)
    key_blocks = keys_all.reshape(key_count, key_block, HEADS, HD)
    value_blocks = values_all.reshape(key_count, key_block, HEADS, HD)
    pos_blocks = all_pos.reshape(key_count, key_block)
    doc_blocks = all_doc.reshape(key_count, key_block)

    def stats_step(carry, block):
        running_top, running_total = carry
        key_part, key_pos, key_doc = block
        raw, allowed = block_scores(query_heads, key_part, own_pos, own_doc, key_pos, key_doc)
        masked = jnp.where(allowed, raw, NEGATIVE)
        new_top = jnp.maximum(running_top, jnp.max(masked, axis=-1))
        terms = jnp.where(allowed, jnp.exp(raw - new_top[..., None]), 0.0)
        running_total = running_total * jnp.exp(running_top - new_top) + jnp.sum(terms, axis=-1)
        return ((new_top, running_total), None)

    start_top = jnp.full((HEADS, local_rows), NEGATIVE, jnp.float32)
    start_total = jnp.zeros((HEADS, local_rows), jnp.float32)
    (final_top, final_total), _ = lax.scan(
        stats_step, (start_top, start_total), (key_blocks, pos_blocks, doc_blocks)
    )
    log_total = final_top + jnp.log(final_total)

    def mix_step(accum, block):
        key_part, value_part, key_pos, key_doc = block
        raw, allowed = block_scores(query_heads, key_part, own_pos, own_doc, key_pos, key_doc)
        probs = jnp.where(allowed, jnp.exp(raw - log_total[..., None]), 0.0).astype(jnp.bfloat16)
        return (
            accum
            + jnp.einsum("hrk,khd->rhd", probs, value_part, preferred_element_type=jnp.float32),
            None,
        )

    mixed, _ = lax.scan(
        mix_step,
        jnp.zeros((local_rows, HEADS, HD), jnp.float32),
        (key_blocks, value_blocks, pos_blocks, doc_blocks),
    )
    attn_low = mixed.reshape(local_rows, D).astype(jnp.bfloat16)
    resid = inputs + jnp.dot(attn_low, out_full, preferred_element_type=jnp.float32)
    normed_two, norm_two_back = jax.vjp(norm_layer, resid, gains[1], biases[1])
    h_two = normed_two.astype(jnp.bfloat16)
    upper = jnp.dot(h_two, up_full, preferred_element_type=jnp.float32)
    active, gelu_back = jax.vjp(gelu_tanh, upper)
    active_low = active.astype(jnp.bfloat16)
    layer_out = (resid + jnp.dot(active_low, down_full, preferred_element_type=jnp.float32)).astype(
        jnp.bfloat16
    )
    regathered = (
        lax.all_gather(norm_gains, "fsdp", axis=1, tiled=True),
        lax.all_gather(norm_biases, "fsdp", axis=1, tiled=True),
        lax.all_gather(w_qkv, "fsdp", axis=0, tiled=True),
        lax.all_gather(w_out, "fsdp", axis=0, tiled=True),
        lax.all_gather(w_up, "fsdp", axis=1, tiled=True),
        lax.all_gather(w_down, "fsdp", axis=0, tiled=True),
    )
    qkv_back = regathered[2]
    out_back = regathered[3]
    up_back = regathered[4]
    down_back = regathered[5]
    cot_low = cotangent[0]
    cot_full = cot_low.astype(jnp.float32)
    down_grad = jnp.dot(active_low.T, cot_low, preferred_element_type=jnp.float32)
    dactive = jnp.dot(cot_low, down_back.T, preferred_element_type=jnp.float32)
    dupper_low = gelu_back(dactive)[0].astype(jnp.bfloat16)
    up_grad = jnp.dot(h_two.T, dupper_low, preferred_element_type=jnp.float32)
    dh_two = jnp.dot(dupper_low, up_back.T, preferred_element_type=jnp.float32)
    dresid_norm, gain_two_grad, bias_two_grad = norm_two_back(dh_two)
    dresid = cot_full + dresid_norm
    dbranch_low = dresid.astype(jnp.bfloat16)
    out_grad = jnp.dot(attn_low.T, dbranch_low, preferred_element_type=jnp.float32)
    dmixed_low = jnp.dot(dbranch_low, out_back.T, preferred_element_type=jnp.float32).astype(
        jnp.bfloat16
    )
    dmixed_heads = dmixed_low.reshape(local_rows, HEADS, HD)
    row_terms = jnp.sum(dmixed_heads.astype(jnp.float32) * mixed, axis=-1).T

    def grad_step(accum, block):
        key_part, value_part, key_pos, key_doc = block
        raw, allowed = block_scores(query_heads, key_part, own_pos, own_doc, key_pos, key_doc)
        probs = jnp.where(allowed, jnp.exp(raw - log_total[..., None]), 0.0)
        dprobs = jnp.einsum(
            "rhd,khd->hrk", dmixed_heads, value_part, preferred_element_type=jnp.float32
        )
        dscore_low = (probs * (dprobs - row_terms[..., None])).astype(jnp.bfloat16)
        accum = accum + jnp.einsum(
            "hrk,khd->rhd", dscore_low, key_part, preferred_element_type=jnp.float32
        )
        dkey_part = jnp.einsum(
            "hrk,rhd->khd", dscore_low, query_heads, preferred_element_type=jnp.float32
        )
        dvalue_part = jnp.einsum(
            "hrk,rhd->khd",
            probs.astype(jnp.bfloat16),
            dmixed_heads,
            preferred_element_type=jnp.float32,
        )
        return (accum, (dkey_part, dvalue_part))

    dquery_sum, (dkey_parts, dvalue_parts) = lax.scan(
        grad_step,
        jnp.zeros((local_rows, HEADS, HD), jnp.float32),
        (key_blocks, value_blocks, pos_blocks, doc_blocks),
    )
    dkeys_all = dkey_parts.reshape(seq_length, D) * scale
    dvalues_all = dvalue_parts.reshape(seq_length, D)
    own_dkeys, own_dvalues = (
        lax.psum_scatter(
            dkeys_all.astype(jnp.bfloat16), "ctx", scatter_dimension=0, tiled=True
        ).astype(jnp.float32),
        lax.psum_scatter(
            dvalues_all.astype(jnp.bfloat16), "ctx", scatter_dimension=0, tiled=True
        ).astype(jnp.float32),
    )
    dquery = dquery_sum.reshape(local_rows, D) * scale
    fresh_width = VH * HD
    first_grad = own_dvalues[:, fresh_width:]
    dqkv_low = jnp.concatenate(
        [
            dquery.astype(jnp.bfloat16),
            own_dkeys.astype(jnp.bfloat16),
            own_dvalues[:, :fresh_width].astype(jnp.bfloat16),
        ],
        axis=1,
    )
    qkv_grad = jnp.dot(h_one.T, dqkv_low, preferred_element_type=jnp.float32)
    dh_one = jnp.dot(dqkv_low, qkv_back.T, preferred_element_type=jnp.float32)
    dinput_norm, gain_one_grad, bias_one_grad = norm_one_back(dh_one)
    input_grad = dresid + dinput_norm
    gain_grads = jnp.stack([gain_one_grad, gain_two_grad])
    bias_grads = jnp.stack([bias_one_grad, bias_two_grad])
    shares = (
        lax.psum_scatter(
            gain_grads.astype(jnp.bfloat16), "fsdp", scatter_dimension=1, tiled=True
        ).astype(jnp.float32),
        lax.psum_scatter(
            bias_grads.astype(jnp.bfloat16), "fsdp", scatter_dimension=1, tiled=True
        ).astype(jnp.float32),
        lax.psum_scatter(
            qkv_grad.astype(jnp.bfloat16), "fsdp", scatter_dimension=0, tiled=True
        ).astype(jnp.float32),
        lax.psum_scatter(
            out_grad.astype(jnp.bfloat16), "fsdp", scatter_dimension=0, tiled=True
        ).astype(jnp.float32),
        lax.psum_scatter(
            up_grad.astype(jnp.bfloat16), "fsdp", scatter_dimension=1, tiled=True
        ).astype(jnp.float32),
        lax.psum_scatter(
            down_grad.astype(jnp.bfloat16), "fsdp", scatter_dimension=0, tiled=True
        ).astype(jnp.float32),
    )
    summed = (
        lax.psum(shares[0].astype(jnp.bfloat16), ("dp", "ctx")).astype(jnp.float32),
        lax.psum(shares[1].astype(jnp.bfloat16), ("dp", "ctx")).astype(jnp.float32),
        lax.psum(shares[2].astype(jnp.bfloat16), ("dp", "ctx")).astype(jnp.float32),
        lax.psum(shares[3].astype(jnp.bfloat16), ("dp", "ctx")).astype(jnp.float32),
        lax.psum(shares[4].astype(jnp.bfloat16), ("dp", "ctx")).astype(jnp.float32),
        lax.psum(shares[5].astype(jnp.bfloat16), ("dp", "ctx")).astype(jnp.float32),
    )
    return (
        layer_out[None],
        input_grad[None],
        first_grad[None],
        summed[0],
        summed[1],
        summed[2],
        summed[3],
        summed[4],
        summed[5],
    )


BLK = 256
GW = 3 * HD
LOG2E = 1.4426950408889634


def block_rows(index):
    return pl.ds(pl.multiple_of(index, BLK), BLK)


def attn_fwd_kernel(
    roff, jmin, start_ref, qkv_ref, p0, p1, p2, p3, ot_ref, lse_ref, o_ref, vt_ref, m_ref, l_ref, acc_ref
):
    blocks = qkv_ref.shape[0] // BLK
    factor = HD ** (-0.5) * LOG2E
    iota_k = lax.broadcasted_iota(jnp.int32, (BLK, BLK), 0)
    iota_q = lax.broadcasted_iota(jnp.int32, (BLK, BLK), 1)

    def flip(p, carry):
        rows = block_rows(roff[p])
        for h in range(3):
            vt_ref[h, p] = qkv_ref[rows, 2 * GW + h * HD : 2 * GW + (h + 1) * HD].T
        return carry

    lax.fori_loop(0, blocks, flip, 0)

    def query_block(i, carry):
        rows = block_rows(roff[i])
        start = start_ref[pl.ds(i, 1), :]
        qts = [qkv_ref[rows, h * HD : (h + 1) * HD].T for h in range(3)]
        for h in range(3):
            m_ref[h] = jnp.full((1, BLK), NEGATIVE, jnp.float32)
            l_ref[h] = jnp.zeros((1, BLK), jnp.float32)
            acc_ref[h] = jnp.zeros((HD, BLK), jnp.float32)

        def step(j, causal):
            krows = block_rows(roff[j])
            allowed = iota_k + j * BLK >= start
            if causal:
                allowed = allowed & (iota_k <= iota_q)
            for h in range(3):
                kh = qkv_ref[krows, GW + h * HD : GW + (h + 1) * HD]
                st = jnp.dot(kh, qts[h], preferred_element_type=jnp.float32) * factor
                st = jnp.where(allowed, st, NEGATIVE)
                m_old = m_ref[h]
                m_new = jnp.maximum(m_old, jnp.max(st, axis=0, keepdims=True))
                pt = jnp.exp2(st - m_new)
                alpha = jnp.exp2(m_old - m_new)
                m_ref[h] = m_new
                l_ref[h] = l_ref[h] * alpha + jnp.sum(pt, axis=0, keepdims=True)
                acc_ref[h] = acc_ref[h] * alpha + jnp.dot(
                    vt_ref[h, j], pt.astype(jnp.bfloat16), preferred_element_type=jnp.float32
                )

        def off_diagonal(j, c):
            step(j, False)
            return c

        lax.fori_loop(jmin[i], i, off_diagonal, 0)
        step(i, True)
        for h in range(3):
            total = l_ref[h]
            ot = acc_ref[h] / total
            ot_ref[h, i] = ot
            lse_ref[h, pl.ds(i, 1), :] = m_ref[h] + jnp.log2(total)
            o_ref[rows, h * HD : (h + 1) * HD] = ot.T.astype(jnp.bfloat16)
        return carry

    lax.fori_loop(0, blocks, query_block, 0)
    for s, piece in enumerate((p0, p1, p2, p3)):
        for b in range(2):
            piece[:, b * GW : (b + 1) * GW] = o_ref[(2 * s + b) * BLK : (2 * s + b + 1) * BLK, :]


def attn_bwd_kernel(
    roff, jmin, start_ref, qkv_ref, d0, d1, d2, d3, ot_ref, lse_ref, out_ref, p0, p1, p2, p3,
    do_ref, kt_ref, dqt_ref, dk_ref, dv_ref,
):
    blocks = qkv_ref.shape[0] // BLK
    scale = HD ** (-0.5)
    factor = scale * LOG2E
    iota_k = lax.broadcasted_iota(jnp.int32, (BLK, BLK), 0)
    iota_q = lax.broadcasted_iota(jnp.int32, (BLK, BLK), 1)

    for s, piece in enumerate((d0, d1, d2, d3)):
        for b in range(2):
            do_ref[(2 * s + b) * BLK : (2 * s + b + 1) * BLK, :] = piece[:, b * GW : (b + 1) * GW]

    def prepare(p, carry):
        rows = block_rows(roff[p])
        for h in range(3):
            kt_ref[h, p] = qkv_ref[rows, GW + h * HD : GW + (h + 1) * HD].T
            dk_ref[h, p] = jnp.zeros((BLK, HD), jnp.float32)
            dv_ref[h, p] = jnp.zeros((BLK, HD), jnp.float32)
        return carry

    lax.fori_loop(0, blocks, prepare, 0)

    def query_block(i, carry):
        rows = block_rows(roff[i])
        start = start_ref[pl.ds(i, 1), :]
        qs = [qkv_ref[rows, h * HD : (h + 1) * HD] for h in range(3)]
        qts = [q.T for q in qs]
        dos = [do_ref[rows, h * HD : (h + 1) * HD] for h in range(3)]
        dots = [d.T for d in dos]
        lses = [lse_ref[h, pl.ds(i, 1), :] for h in range(3)]
        deltas = [
            jnp.sum(dots[h].astype(jnp.float32) * ot_ref[h, i], axis=0, keepdims=True)
            for h in range(3)
        ]
        for h in range(3):
            dqt_ref[h] = jnp.zeros((HD, BLK), jnp.float32)

        def step(j, causal):
            krows = block_rows(roff[j])
            allowed = iota_k + j * BLK >= start
            if causal:
                allowed = allowed & (iota_k <= iota_q)
            for h in range(3):
                kh = qkv_ref[krows, GW + h * HD : GW + (h + 1) * HD]
                vh = qkv_ref[krows, 2 * GW + h * HD : 2 * GW + (h + 1) * HD]
                st = jnp.dot(kh, qts[h], preferred_element_type=jnp.float32)
                dpt = jnp.dot(vh, dots[h], preferred_element_type=jnp.float32)
                pt = jnp.where(allowed, jnp.exp2(st * factor - lses[h]), 0.0)
                dst = (pt * (dpt - deltas[h])).astype(jnp.bfloat16)
                dv_ref[h, j] += jnp.dot(
                    pt.astype(jnp.bfloat16), dos[h], preferred_element_type=jnp.float32
                )
                dk_ref[h, j] += jnp.dot(dst, qs[h], preferred_element_type=jnp.float32)
                dqt_ref[h] += jnp.dot(kt_ref[h, j], dst, preferred_element_type=jnp.float32)

        def off_diagonal(j, c):
            step(j, False)
            return c

        lax.fori_loop(jmin[i], i, off_diagonal, 0)
        step(i, True)
        for h in range(3):
            out_ref[rows, h * HD : (h + 1) * HD] = (dqt_ref[h] * scale).T.astype(jnp.bfloat16)
        return carry

    lax.fori_loop(0, blocks, query_block, 0)

    def finish(p, carry):
        rows = block_rows(roff[p])
        for h in range(3):
            out_ref[rows, GW + h * HD : GW + (h + 1) * HD] = (dk_ref[h, p] * scale).astype(
                jnp.bfloat16
            )
            out_ref[rows, 2 * GW + h * HD : 2 * GW + (h + 1) * HD] = dv_ref[h, p].astype(
                jnp.bfloat16
            )
        return carry

    lax.fori_loop(0, blocks, finish, 0)
    for s, piece in enumerate((p0, p1, p2, p3)):
        for b in range(2):
            piece[:, 3 * b * GW : 3 * (b + 1) * GW] = out_ref[(2 * s + b) * BLK : (2 * s + b + 1) * BLK, :]


SMEM_SPEC = pl.BlockSpec(memory_space=pltpu.SMEM)
VMEM_SPEC = pl.BlockSpec(memory_space=pltpu.VMEM)


def attn_forward(roff, jmin, starts, qkv):
    length = qkv.shape[0]
    blocks = length // BLK
    return pl.pallas_call(
        attn_fwd_kernel,
        name="attn_forward",
        out_shape=(
            *[jax.ShapeDtypeStruct((BLK, 2 * GW), jnp.bfloat16)] * 4,
            jax.ShapeDtypeStruct((3, blocks, HD, BLK), jnp.float32),
            jax.ShapeDtypeStruct((3, blocks, BLK), jnp.float32),
        ),
        in_specs=[SMEM_SPEC, SMEM_SPEC, VMEM_SPEC, VMEM_SPEC],
        out_specs=(VMEM_SPEC,) * 6,
        scratch_shapes=[
            pltpu.VMEM((length, GW), jnp.bfloat16),
            pltpu.VMEM((3, blocks, HD, BLK), jnp.bfloat16),
            pltpu.VMEM((3, 1, BLK), jnp.float32),
            pltpu.VMEM((3, 1, BLK), jnp.float32),
            pltpu.VMEM((3, HD, BLK), jnp.float32),
        ],
    )(roff, jmin, starts, qkv)


def attn_backward(roff, jmin, starts, qkv, dout, ot, lse):
    length = qkv.shape[0]
    blocks = length // BLK
    return pl.pallas_call(
        attn_bwd_kernel,
        name="attn_backward",
        out_shape=(
            jax.ShapeDtypeStruct((length, 3 * GW), jnp.bfloat16),
            *[jax.ShapeDtypeStruct((BLK, 6 * GW), jnp.bfloat16)] * 4,
        ),
        in_specs=[SMEM_SPEC, SMEM_SPEC] + [VMEM_SPEC] * 8,
        out_specs=(VMEM_SPEC,) * 5,
        scratch_shapes=[
            pltpu.VMEM((length, GW), jnp.bfloat16),
            pltpu.VMEM((3, blocks, HD, BLK), jnp.bfloat16),
            pltpu.VMEM((3, HD, BLK), jnp.float32),
            pltpu.VMEM((3, blocks, BLK, HD), jnp.float32),
            pltpu.VMEM((3, blocks, BLK, HD), jnp.float32),
        ],
    )(roff, jmin, starts, qkv, *dout, ot, lse)


def unit_of(values_in):
    center = jnp.mean(values_in, axis=-1, keepdims=True)
    centred = values_in - center
    spread = lax.rsqrt(jnp.mean(centred * centred, axis=-1, keepdims=True) + EPSILON)
    return centred * spread, spread


def norm_back(grad, unit, spread, gain):
    scaled = grad * gain
    return spread * (
        scaled
        - jnp.mean(scaled, axis=-1, keepdims=True)
        - unit * jnp.mean(scaled * unit, axis=-1, keepdims=True)
    )


def project_kernel(ids, xa, xb, w_ref, lines, first, *rest):
    unit_out, qkv_out = rest[-2], rest[-1]
    weights = w_ref[0]
    reuse = ids[1] == 1
    for b, x_ref in enumerate((xa, xb)):
        unit, _ = unit_of(x_ref[...].astype(jnp.float32))
        normed = (unit * lines[0:1, :] + lines[2:3, :]).astype(jnp.bfloat16)
        part = jnp.dot(normed, weights, preferred_element_type=jnp.float32).astype(jnp.bfloat16)
        here = slice(b * BLK, (b + 1) * BLK)
        qkv_out[here, : 2 * GW] = part[:, : 2 * GW]
        qkv_out[here, 2 * GW :] = jnp.where(reuse, first[:, b * GW : (b + 1) * GW], part[:, 2 * GW :])
        unit_out[:, here] = unit.astype(jnp.bfloat16).T


def project(slot, ids, xa, xb, grouped, lines, first, held):
    length = 8 * BLK
    whole = lambda *shape: pl.BlockSpec(shape, lambda i, ids_ref: (0,) * len(shape))
    in_specs = [
        whole(BLK, D),
        whole(BLK, D),
        pl.BlockSpec((1, D, 3 * GW), lambda i, ids_ref: (ids_ref[0], 0, 0)),
        whole(4, D),
        whole(BLK, 2 * GW),
    ]
    args = [ids, xa, xb, grouped, lines, first]
    aliases = {}
    if held is not None:
        in_specs += [pl.BlockSpec(memory_space=pl.ANY)] * 2
        aliases = {6: 0, 7: 1}
        args += list(held)
    return pl.pallas_call(
        project_kernel,
        name="project_" + str(slot),
        grid_spec=pltpu.PrefetchScalarGridSpec(
            num_scalar_prefetch=1,
            grid=(1,),
            in_specs=in_specs,
            out_specs=(
                pl.BlockSpec((D, 2 * BLK), lambda i, ids_ref: (0, slot)),
                pl.BlockSpec((2 * BLK, 3 * GW), lambda i, ids_ref: (slot, 0)),
            ),
        ),
        out_shape=(
            jax.ShapeDtypeStruct((D, length), jnp.bfloat16),
            jax.ShapeDtypeStruct((length, 3 * GW), jnp.bfloat16),
        ),
        input_output_aliases=aliases,
    )(*args)


def resid_kernel(groups, x_ref, m0, m1, m2, m3, w_ref, lines, resid_ref, h_ref, attn_ref):
    for b in range(2):
        here = slice(b * BLK, (b + 1) * BLK)
        for s, piece in enumerate((m0, m1, m2, m3)):
            attn_ref[here, s * GW : (s + 1) * GW] = piece[:, b * GW : (b + 1) * GW]
        total = x_ref[here, :].astype(jnp.float32)
        for s, piece in enumerate((m0, m1, m2, m3)):
            rows = pl.ds(pl.multiple_of(groups[s] * GW, GW), GW)
            total += jnp.dot(
                piece[:, b * GW : (b + 1) * GW], w_ref[rows, :], preferred_element_type=jnp.float32
            )
        resid_ref[here, :] = total
        unit, _ = unit_of(total)
        h_ref[here, :] = (unit * lines[1:2, :] + lines[3:4, :]).astype(jnp.bfloat16)


def residual(groups, x, pieces, out_full, lines):
    rows = x.shape[0]
    return pl.pallas_call(
        resid_kernel,
        name="residual",
        out_shape=(
            jax.ShapeDtypeStruct((rows, D), jnp.float32),
            jax.ShapeDtypeStruct((rows, D), jnp.bfloat16),
            jax.ShapeDtypeStruct((rows, D), jnp.bfloat16),
        ),
        in_specs=[SMEM_SPEC] + [VMEM_SPEC] * 7,
        out_specs=(VMEM_SPEC,) * 3,
    )(groups, x, *pieces, out_full, lines)


ROOT = 0.7978845608028654
TILE = 256


def feed_kernel(ha, hb, dact, um, uo, gm, go, dum, duo, dh_own, dh_far, acc):
    t = pl.program_id(0)
    half = pl.num_programs(0) // 2
    rows = ha.shape[0]

    @pl.when(t == 0)
    def _():
        acc[...] = jnp.zeros_like(acc)

    def tile(up_ref, g_out, du_out):
        weights = up_ref[...]
        for r in range(2 * rows // TILE):
            src = ha if r * TILE < rows else hb
            at = (r * TILE) % rows
            here = slice(r * TILE, (r + 1) * TILE)
            u = jnp.dot(src[at : at + TILE, :], weights, preferred_element_type=jnp.float32)
            squared = u * u
            tanned = jnp.tanh(ROOT * u * (1.0 + 0.044715 * squared))
            inner = 0.5 + 0.5 * tanned
            g_out[here, :] = (u * inner).astype(jnp.bfloat16)
            slope = inner + u * (0.5 - 0.5 * tanned * tanned) * (ROOT + (3.0 * 0.044715 * ROOT) * squared)
            du = (dact[here, :].astype(jnp.float32) * slope).astype(jnp.bfloat16)
            du_out[here, :] = du
            acc[here, :] += lax.dot_general(
                du, weights, (((1,), (1,)), ((), ())), preferred_element_type=jnp.float32
            )

    @pl.when(t < half)
    def _():
        tile(um, gm, dum)

    @pl.when(t >= half)
    def _():
        tile(uo, go, duo)

    @pl.when(t == pl.num_programs(0) - 1)
    def _():
        dh_own[...] = acc[:rows, :]
        dh_far[...] = acc[rows:, :].astype(jnp.bfloat16)


def feed(ha, hb, dact, up_mine, up_other):
    rows = ha.shape[0]
    width = up_mine.shape[1]
    steps = width // TILE
    whole = lambda *shape: pl.BlockSpec(shape, lambda t: (0,) * len(shape))
    early = lambda t: jnp.minimum(t, steps - 1)
    late = lambda t: jnp.maximum(t - steps, 0)
    wide = lambda pick: pl.BlockSpec((2 * rows, TILE), lambda t: (0, pick(t)))
    return pl.pallas_call(
        feed_kernel,
        name="feed",
        grid=(2 * steps,),
        out_shape=(
            *[jax.ShapeDtypeStruct((2 * rows, width), jnp.bfloat16)] * 4,
            jax.ShapeDtypeStruct((rows, D), jnp.float32),
            jax.ShapeDtypeStruct((rows, D), jnp.bfloat16),
        ),
        in_specs=[
            whole(rows, D),
            whole(rows, D),
            pl.BlockSpec((2 * rows, TILE), lambda t: (0, t)),
            pl.BlockSpec((D, TILE), lambda t: (0, early(t))),
            pl.BlockSpec((D, TILE), lambda t: (0, late(t))),
        ],
        out_specs=(wide(early), wide(late), wide(early), wide(late), whole(rows, D), whole(rows, D)),
        scratch_shapes=[pltpu.VMEM((2 * rows, D), jnp.float32)],
    )(ha, hb, dact, up_mine, up_other)


def branch_kernel(groups, dh_ref, far_ref, resid_ref, cot_ref, lines, w_ref, dresid_ref, low_ref, p0, p1, p2, p3, sums):
    gain_sum = jnp.zeros((1, D), jnp.float32)
    bias_sum = jnp.zeros((1, D), jnp.float32)
    for b in range(2):
        here = slice(b * BLK, (b + 1) * BLK)
        unit, spread = unit_of(resid_ref[here, :])
        grad = dh_ref[here, :] + far_ref[here, :].astype(jnp.float32)
        gain_sum += jnp.sum(grad * unit, axis=0, keepdims=True)
        bias_sum += jnp.sum(grad, axis=0, keepdims=True)
        total = cot_ref[here, :].astype(jnp.float32) + norm_back(grad, unit, spread, lines[1:2, :])
        dresid_ref[here, :] = total
        low = total.astype(jnp.bfloat16)
        low_ref[here, :] = low
        for s, piece in enumerate((p0, p1, p2, p3)):
            rows = pl.ds(pl.multiple_of(groups[s] * GW, GW), GW)
            piece[:, b * GW : (b + 1) * GW] = lax.dot_general(
                low, w_ref[rows, :], (((1,), (1,)), ((), ())), preferred_element_type=jnp.float32
            ).astype(jnp.bfloat16)
    sums[0:1, :] = gain_sum
    sums[1:2, :] = bias_sum


def branch(groups, dh, far, resid, cot, lines, out_full):
    rows = dh.shape[0]
    return pl.pallas_call(
        branch_kernel,
        name="branch",
        out_shape=(
            jax.ShapeDtypeStruct((rows, D), jnp.float32),
            jax.ShapeDtypeStruct((rows, D), jnp.bfloat16),
            *[jax.ShapeDtypeStruct((BLK, 2 * GW), jnp.bfloat16)] * 4,
            jax.ShapeDtypeStruct((2, D), jnp.float32),
        ),
        in_specs=[SMEM_SPEC] + [VMEM_SPEC] * 6,
        out_specs=(VMEM_SPEC,) * 7,
    )(groups, dh, far, resid, cot, lines, out_full)


def product_kernel(ids, unit_ref, dqkv_ref, w_ref, lines, sums2, out_ref):
    weights = w_ref[0].astype(jnp.float32)
    columns = lines[...].T
    two = sums2[...].T
    column_sums = jnp.sum(dqkv_ref[...].astype(jnp.float32), axis=0, keepdims=True)
    zeros = jnp.zeros((BLK, 60), jnp.float32)
    for r in range(D // BLK):
        here = slice(r * BLK, (r + 1) * BLK)
        product = jnp.dot(unit_ref[here, :], dqkv_ref[...], preferred_element_type=jnp.float32)
        w = weights[here, :]
        gain_col = jnp.sum(w * product, axis=1, keepdims=True)
        bias_col = jnp.sum(w * column_sums, axis=1, keepdims=True)
        out_ref[here, : 3 * GW] = columns[here, 0:1] * product + columns[here, 2:3] * column_sums
        out_ref[here, 3 * GW :] = jnp.concatenate(
            [gain_col, two[here, 0:1], bias_col, two[here, 1:2], zeros], axis=1
        )


def qkv_product(ids, unit_t, dqkv, grouped, lines, sums2):
    whole = lambda *shape: pl.BlockSpec(shape, lambda i, ids_ref: (0,) * len(shape))
    length = dqkv.shape[0]
    return pl.pallas_call(
        product_kernel,
        name="qkv_product",
        grid_spec=pltpu.PrefetchScalarGridSpec(
            num_scalar_prefetch=1,
            grid=(1,),
            in_specs=[
                whole(D, length),
                whole(length, 3 * GW),
                pl.BlockSpec((1, D, 3 * GW), lambda i, ids_ref: (ids_ref[0], 0, 0)),
                whole(4, D),
                whole(2, D),
            ],
            out_specs=whole(D, 3 * GW + 64),
        ),
        out_shape=jax.ShapeDtypeStruct((D, 3 * GW + 64), jnp.float32),
    )(ids, unit_t, dqkv, grouped, lines, sums2)


def input_kernel(groups, place, x_ref, dresid_ref, b0, b1, b2, b3, w_ref, lines, out_ref, first_ref):
    pieces = (b0, b1, b2, b3)
    for b in range(2):
        here = slice(b * BLK, (b + 1) * BLK)
        wide = slice(3 * b * GW, 3 * (b + 1) * GW)
        grad = jnp.zeros((BLK, D), jnp.float32)
        for s, piece in enumerate(pieces):
            grad += lax.dot_general(
                piece[:, wide], w_ref[groups[s]], (((1,), (1,)), ((), ())), preferred_element_type=jnp.float32
            )
        unit, spread = unit_of(x_ref[here, :].astype(jnp.float32))
        out_ref[here, :] = dresid_ref[here, :] + norm_back(grad, unit, spread, lines[0:1, :])
        values = slice(3 * b * GW + 2 * GW, 3 * (b + 1) * GW)
        for k in range(2):
            total = jnp.zeros((BLK, GW), jnp.float32)
            for s, piece in enumerate(pieces):
                total = jnp.where(place[2 + k] == s, piece[:, values].astype(jnp.float32), total)
            first_ref[here, k * GW : (k + 1) * GW] = total


def input_gradient(groups, place, x, dresid, pieces, grouped, lines):
    rows = x.shape[0]
    return pl.pallas_call(
        input_kernel,
        name="input_gradient",
        out_shape=(
            jax.ShapeDtypeStruct((rows, D), jnp.float32),
            jax.ShapeDtypeStruct((rows, 2 * GW), jnp.float32),
        ),
        in_specs=[SMEM_SPEC, SMEM_SPEC] + [VMEM_SPEC] * 8,
        out_specs=(VMEM_SPEC,) * 2,
    )(groups, place, x, dresid, *pieces, grouped, lines)


def after(value, *others):
    return lax.optimization_barrier((value,) + others)[0]


def shift_ctx(value, shift):
    return lax.ppermute(value, "ctx", [(i, (i + shift) % 4) for i in range(4)])


def swap_core(value):
    return lax.ppermute(value, "fsdp", [(i, i ^ 1) for i in range(4)])


def swap_x(value):
    return lax.ppermute(value, "fsdp", [(i, i ^ 2) for i in range(4)])


def swap_dp(value):
    return lax.ppermute(value, "dp", [(0, 1), (1, 0)])


def in_fsdp_order(index, own, other, pair):
    stacked = jnp.concatenate([own[None], other[None], pair])
    return [
        lax.dynamic_index_in_dim(stacked, order_of(index, wanted), 0, keepdims=False)
        for wanted in range(4)
    ]


def order_of(index, wanted):
    apart = jnp.bitwise_xor(index, wanted)
    return (apart >> 1) + 2 * (apart & 1)


def dot32(a, b):
    return jnp.dot(a, b, preferred_element_type=jnp.float32)


def dot_nt(a, b):
    return lax.dot_general(a, b, (((1,), (1,)), ((), ())), preferred_element_type=jnp.float32)


def dot_tn(a, b):
    return lax.dot_general(a, b, (((0,), (0,)), ((), ())), preferred_element_type=jnp.float32)


GROUP_OF = (0, 2, 3, 1)


def pick(table, index):
    return sum(jnp.where(index == k, entry, 0) for k, entry in enumerate(table)).astype(jnp.int32)


def grouped_body(
    layer_input,
    first_values,
    segment_ids,
    pairing,
    norm_gains,
    norm_biases,
    w_qkv,
    w_out,
    w_up,
    w_down,
    cotangent,
):
    ctx = lax.axis_index("ctx")
    fsdp = lax.axis_index("fsdp")
    rows = layer_input.shape[1]
    length = rows * 4
    blocks = length // BLK
    turns = jnp.arange(4, dtype=jnp.int32)
    groups = pick(GROUP_OF, (ctx + turns) % 4)
    place = (pick([GROUP_OF.index(g) for g in range(4)], turns) - ctx) % 4
    reuses = ((ctx == 1) | (ctx == 2)).astype(jnp.int32)
    ids = jnp.stack([groups[0], reuses])

    doc_row = segment_ids[0]
    starts = jnp.sum(
        (doc_row[None, :] < doc_row[:, None]).astype(jnp.int32), axis=1, dtype=jnp.int32
    ).reshape(blocks, BLK)
    firsts, lasts = doc_row[::BLK], doc_row[BLK - 1 :: BLK]
    jmin = jnp.sum((lasts[None, :] < firsts[:, None]).astype(jnp.int32), axis=1, dtype=jnp.int32)
    block_ids = jnp.arange(blocks, dtype=jnp.int32)
    held_at = jnp.sum(
        jnp.where(pairing[None, :] == block_ids[:, None], block_ids[None, :], 0), axis=1, dtype=jnp.int32
    )
    roff = ((ctx - held_at // 2) % 4) * rows + (held_at % 2) * BLK

    chunk = layer_input[0]
    xa, xb = chunk[:BLK], chunk[BLK:]
    qkv_other = swap_x(w_qkv)
    ring_a, ring_b = [xa, shift_ctx(xa, 1)], [xb, shift_ctx(xb, 1)]

    first = first_values[0]
    message = [
        jnp.concatenate([first[:BLK, k * GW : (k + 1) * GW], first[BLK:, k * GW : (k + 1) * GW]], axis=1)
        for k in range(2)
    ]
    first_parts = [jnp.where(ctx == 1, message[0], message[1])]
    for s in range(1, 4):
        pairs = [(i, (i + s) % 4) for i in range(4) if (i + s) % 4 in (1, 2)]
        first_parts.append(
            lax.ppermute(jnp.where((ctx + s) % 4 == 1, message[0], message[1]), "ctx", pairs)
        )

    norms = jnp.pad(jnp.concatenate([norm_gains, norm_biases], axis=0), ((0, 12), (0, D - D // 4)))
    out_norms = jnp.concatenate([w_out, norms], axis=0)
    out_other = swap_x(out_norms)
    cot_own = cotangent[0]
    cot_far = swap_core(cot_own)

    ring_a.append(shift_ctx(ring_a[1], 1))
    ring_b.append(shift_ctx(ring_b[1], 1))
    qkv_pair = swap_core(after(jnp.stack([w_qkv, qkv_other]), ring_a[1], ring_b[1]))
    out_pair = swap_core(jnp.stack([out_norms, out_other]))
    down_other = swap_x(after(w_down, qkv_other))
    up_other = swap_x(after(w_up, qkv_other))
    qkv_full = jnp.concatenate(in_fsdp_order(fsdp, w_qkv, qkv_other, qkv_pair), axis=0)
    out_parts = in_fsdp_order(fsdp, out_norms, out_other, out_pair)
    out_full = jnp.concatenate([part[: D // 4] for part in out_parts], axis=0)
    lines = jnp.concatenate(
        [part[D // 4 : D // 4 + 4, : D // 4] for part in out_parts], axis=1
    ).astype(jnp.float32)
    grouped = []
    for g in range(4):
        wv = (
            qkv_full[:, 2 * D + g * GW : 2 * D + (g + 1) * GW]
            if (g + 1) * GW <= VH * HD
            else jnp.zeros((D, GW), jnp.bfloat16)
        )
        grouped.append(
            jnp.concatenate(
                [qkv_full[:, g * GW : (g + 1) * GW], qkv_full[:, D + g * GW : D + (g + 1) * GW], wv],
                axis=1,
            )
        )
    grouped = jnp.stack(grouped)
    ring_a.append(shift_ctx(ring_a[2], 1))
    ring_b.append(shift_ctx(ring_b[2], 1))

    held = None
    for s in range(4):
        held = project(s, ids, ring_a[s], ring_b[s], grouped, lines, first_parts[s], held)
    unit_t, qkv_heads = held

    forward = attn_forward(roff, jmin, starts, qkv_heads)
    mixed, mixed_t, lse = forward[:4], forward[4], forward[5]
    pieces = [mixed[0]] + [shift_ctx(mixed[s], -s) for s in range(1, 4)]
    cot_both = after(jnp.concatenate([cot_own, cot_far], axis=0), mixed[0])
    dactive = jnp.concatenate([dot_nt(cot_both, w_down), dot_nt(cot_both, down_other)], axis=1).astype(
        jnp.bfloat16
    )
    resid, h_two, attn_low = residual(groups, chunk, pieces, out_full, lines)
    h_far = swap_core(h_two)
    g_mine, g_other, du_mine, du_other, dh_own, dh_far = feed(h_two, h_far, dactive, w_up, up_other)
    dh_back = swap_core(dh_far)
    dresid, dbranch_low, d0, d1, d2, d3, sums2 = branch(
        groups, dh_own, dh_back, resid, cot_own, lines, out_full
    )
    dmixed = [d0] + [shift_ctx(d, s) for s, d in ((1, d1), (2, d2), (3, d3))]

    g_other, du_other, g_mine, du_mine = lax.optimization_barrier(
        (g_other, du_other, g_mine, du_mine, d1)
    )[:4]
    h_both = jnp.concatenate([h_two, h_far], axis=0)
    down_far = swap_x(dot_tn(g_other, cot_both).astype(jnp.bfloat16))
    up_far = swap_x(dot_tn(h_both, du_other).astype(jnp.bfloat16))
    out_turned_grad = dot_tn(attn_low, dbranch_low)
    out_shares = out_turned_grad.reshape(4, GW, D)
    out_sum = reduce_fsdp(
        jnp.stack(
            [lax.dynamic_index_in_dim(out_shares, place[g], 0, keepdims=False) for g in range(4)]
        ),
        fsdp,
    )
    down_mine = dot_tn(g_mine, cot_both)
    up_mine = dot_tn(h_both, du_mine)
    down_sum = down_mine + down_far.astype(jnp.float32)
    up_sum = up_mine + up_far.astype(jnp.float32)
    down_low, up_low, out_low = lax.psum(
        (down_sum.astype(jnp.bfloat16), up_sum.astype(jnp.bfloat16), out_sum.astype(jnp.bfloat16)),
        ("dp", "ctx"),
    )
    out_both = dot32(g_mine, w_down) + dot32(g_other, down_other)
    layer_out = (
        resid + out_both[:rows] + swap_core(out_both[rows:].astype(jnp.bfloat16)).astype(jnp.float32)
    ).astype(jnp.bfloat16)

    backward = attn_backward(roff, jmin, starts, qkv_heads, dmixed, mixed_t, lse)
    dqkv = backward[0]
    back = [backward[1]] + [shift_ctx(backward[1 + s], -s) for s in range(1, 4)]

    share = qkv_product(ids, unit_t, dqkv, grouped, lines, sums2).reshape(4, D // 4, 3 * GW + 64)
    share = reduce_fsdp(share, fsdp)
    share_low = share.astype(jnp.bfloat16)
    share_low = (share + swap_dp(share_low).astype(jnp.float32)).astype(jnp.bfloat16)
    others = jnp.stack([share_low] + [shift_ctx(share_low, -s) for s in range(1, 4)])
    by_group = [
        lax.dynamic_index_in_dim(others, place[g], 0, keepdims=False).astype(jnp.float32)
        for g in range(4)
    ]
    qkv_grad = jnp.concatenate(
        [b[:, :GW] for b in by_group]
        + [b[:, GW : 2 * GW] for b in by_group]
        + [by_group[g][:, 2 * GW : 3 * GW] for g in range(2)],
        axis=1,
    )
    norm_grads = sum(b[:, 3 * GW : 3 * GW + 4] for b in by_group).T
    gains_grad, biases_grad = norm_grads[:2], norm_grads[2:4]

    input_grad, first_grad = input_gradient(groups, place, chunk, dresid, back, grouped, lines)

    return (
        layer_out[None],
        input_grad[None],
        first_grad[None],
        gains_grad,
        biases_grad,
        qkv_grad,
        out_low.astype(jnp.float32),
        up_low.astype(jnp.float32),
        down_low.astype(jnp.float32),
    )


def reduce_fsdp(shares, fsdp):
    turned = shares.reshape((2, 2) + shares.shape[1:])
    core = fsdp % 2
    x = fsdp // 2
    keep = lax.dynamic_index_in_dim(turned, core, 1, keepdims=False)
    give = lax.dynamic_index_in_dim(turned, 1 - core, 1, keepdims=False)
    pair = keep + swap_core(give.astype(jnp.bfloat16)).astype(jnp.float32)
    mine = lax.dynamic_index_in_dim(pair, x, 0, keepdims=False)
    other = lax.dynamic_index_in_dim(pair, 1 - x, 0, keepdims=False)
    return mine + swap_x(other.astype(jnp.bfloat16)).astype(jnp.float32)


def solution(mesh):
    sizes = dict(mesh.shape)
    small = sizes["dp"] == 2 and sizes["ctx"] == 4 and sizes["fsdp"] == 4
    chosen = grouped_body if small else wide_body
    in_specs = (
        P(("dp", "fsdp"), "ctx", None),
        P(("dp", "fsdp"), "ctx", None),
        P(("dp", "fsdp"), None),
        P(),
        P(None, "fsdp"),
        P(None, "fsdp"),
        P("fsdp", None),
        P("fsdp", None),
        P(None, "fsdp"),
        P("fsdp", None),
        P(("dp", "fsdp"), "ctx", None),
    )
    out_specs = (
        P(("dp", "fsdp"), "ctx", None),
        P(("dp", "fsdp"), "ctx", None),
        P(("dp", "fsdp"), "ctx", None),
        P(None, "fsdp"),
        P(None, "fsdp"),
        P("fsdp", None),
        P("fsdp", None),
        P(None, "fsdp"),
        P("fsdp", None),
    )
    return jax.shard_map(chosen, mesh=mesh, in_specs=in_specs, out_specs=out_specs, check_vma=False)
```
